32 devices in a mesh: tm: 8 (over y, x, core), space: 4 (over z).
Axes of the slice: x: 2, y: 2, z: 4, core: 2. Of those that a mesh axis runs over, the one named last changes fastest.
Arguments:
- frames: bfloat16 [128, 256, 768], P('tm', 'space'), may hold values from -6 to 6
- gain_time: float32 [768], replicated, may hold values from 0.25 to 1.75
- wq_time: bfloat16 [768, 768], replicated, may hold values from -6 to 6
- wkv_time: bfloat16 [768, 512], replicated, may hold values from -6 to 6
- wo_time: bfloat16 [768, 768], replicated, may hold values from -0.21875 to 0.21875
- gain_space: float32 [768], replicated, may hold values from 0.25 to 1.75
- wq_space: bfloat16 [768, 768], replicated, may hold values from -6 to 6
- wkv_space: bfloat16 [768, 512], replicated, may hold values from -6 to 6
- wo_space: bfloat16 [768, 768], replicated, may hold values from -0.21875 to 0.21875
- gain_mlp: float32 [768], replicated, may hold values from 0.25 to 1.75
- w_in: bfloat16 [768, 3072], replicated, may hold values from -0.21875 to 0.21875
- w_out: bfloat16 [3072, 768], replicated, may hold values from -0.109375 to 0.109375
Outputs:
- encoded: bfloat16 [128, 256, 768], P('tm', 'space')
The draws below stay inside these ranges and needn't reach their ends.
All inputs are finite; a program needn't handle non-finite values.
Results may differ from the reference program's by a relative error of at most 0.025.
The reference program's roundings to bfloat16 on the way count: a program that leaves them out, or rounds other values in their place, can miss the bound.
Values may be sent and summed in bfloat16 or wider, within the bound.
A program may use at most 192 MiB of HBM per device.

```python
import jax
import jax.numpy as jnp
from jax import lax

D = 768
HEADS = 12
KV_HEADS = 4
HEAD = 64
FF = 3072
WINDOW = 8
FRAMES = 128
PATCHES = 256


def projection_pair(key, label):
    base = jax.random.fold_in(key, label)
    first, second, third = jax.random.split(base, 3)
    scale = 1.0 / jnp.sqrt(jnp.float32(D))
    w_query = jax.random.normal(first, (D, HEADS * HEAD), jnp.float32) * scale
    w_keys = jax.random.normal(second, (D, KV_HEADS * HEAD), jnp.float32) * scale
    w_values = jax.random.normal(third, (D, KV_HEADS * HEAD), jnp.float32) * scale
    w_query = jnp.clip(w_query, -6.0, 6.0)
    w_both = jnp.clip(jnp.concatenate([w_keys, w_values], axis=1), -6.0, 6.0)
    return (w_query, w_both)


def draw_wq_time(key, part):
    return projection_pair(key, 11)[0].astype(jnp.bfloat16)


def draw_wkv_time(key, part):
    return projection_pair(key, 11)[1].astype(jnp.bfloat16)


def draw_wq_space(key, part):
    return projection_pair(key, 23)[0].astype(jnp.bfloat16)


def draw_wkv_space(key, part):
    return projection_pair(key, 23)[1].astype(jnp.bfloat16)


def draw_frames(key, part):
    values = jax.random.normal(key, (FRAMES, PATCHES, D), jnp.float32)
    return jnp.clip(values, -6.0, 6.0).astype(jnp.bfloat16)


def normal_values(key, extent, width, limit, kind=jnp.bfloat16):
    return jnp.clip(width * jax.random.normal(key, extent, jnp.float32), -limit, limit).astype(kind)


def setup_inputs(seed: int = 0) -> dict:
    arg_keys = jax.random.split(jax.random.key(seed), 13)
    return {
        "frames": draw_frames(jax.random.fold_in(arg_keys[12], 71), 0),
        "gain_time": jnp.clip(1.0 + 0.15 * jax.random.normal(arg_keys[1], (D,), jnp.float32), 0.25, 1.75),
        "wq_time": draw_wq_time(jax.random.fold_in(arg_keys[12], 71), 0),
        "wkv_time": draw_wkv_time(jax.random.fold_in(arg_keys[12], 71), 0),
        "wo_time": normal_values(arg_keys[4], (HEADS * HEAD, D), D ** -0.5, 0.21875),
        "gain_space": jnp.clip(1.0 + 0.15 * jax.random.normal(arg_keys[5], (D,), jnp.float32), 0.25, 1.75),
        "wq_space": draw_wq_space(jax.random.fold_in(arg_keys[12], 71), 0),
        "wkv_space": draw_wkv_space(jax.random.fold_in(arg_keys[12], 71), 0),
        "wo_space": normal_values(arg_keys[8], (HEADS * HEAD, D), D ** -0.5, 0.21875),
        "gain_mlp": jnp.clip(1.0 + 0.15 * jax.random.normal(arg_keys[9], (D,), jnp.float32), 0.25, 1.75),
        "w_in": normal_values(arg_keys[10], (D, FF), D ** -0.5, 0.21875),
        "w_out": normal_values(arg_keys[11], (FF, D), FF ** -0.5, 0.109375),
    }


def layer_norm(x, gain):
    xf = x.astype(jnp.float32)
    mean = lax.optimization_barrier(jnp.mean(xf, axis=-1, keepdims=True))
    var = lax.optimization_barrier(jnp.mean((xf - mean) * (xf - mean), axis=-1, keepdims=True))
    return ((xf - mean) * lax.rsqrt(var + 1e-06) * gain).astype(jnp.bfloat16)

def project(a, w):
    flat = a.reshape(-1, a.shape[-1])
    return jnp.dot(flat, w, preferred_element_type=jnp.float32).reshape(a.shape[:-1] + (w.shape[1],))

def attend_time(query, keys, valid):
    group = HEADS // KV_HEADS
    patches = query.shape[0]
    span = keys.shape[0]
    q_heads = query.reshape(patches, KV_HEADS, group, HEAD).astype(jnp.float32)
    k_heads = keys[..., :KV_HEADS * HEAD].reshape(span, patches, KV_HEADS, HEAD).astype(jnp.float32)
    v_heads = keys[..., KV_HEADS * HEAD:].reshape(span, patches, KV_HEADS, HEAD).astype(jnp.float32)
    scores = jnp.einsum('pgrd,jpgd->pgrj', q_heads, k_heads) / jnp.sqrt(jnp.float32(HEAD))
    scores = jnp.where(valid, scores, jnp.float32(-1e+30))
    top = lax.optimization_barrier(jnp.max(scores, axis=-1, keepdims=True))
    expo = jnp.exp(scores - top)
    weights = (expo / lax.optimization_barrier(jnp.sum(expo, axis=-1, keepdims=True))).astype(jnp.bfloat16)
    out = jnp.einsum('pgrj,jpgd->pgrd', weights.astype(jnp.float32), v_heads)
    return out.reshape(patches, HEADS * HEAD).astype(jnp.bfloat16)

def attend_space(query, keyvals):
    group = HEADS // KV_HEADS
    patches = query.shape[0]
    count = keyvals.shape[0]
    q_heads = query.reshape(patches, KV_HEADS, group, HEAD).astype(jnp.float32)
    k_heads = keyvals[:, :KV_HEADS * HEAD].reshape(count, KV_HEADS, HEAD).astype(jnp.float32)
    v_heads = keyvals[:, KV_HEADS * HEAD:].reshape(count, KV_HEADS, HEAD).astype(jnp.float32)
    scores = jnp.einsum('pgrd,kgd->grpk', q_heads, k_heads) / jnp.sqrt(jnp.float32(HEAD))
    top = lax.optimization_barrier(jnp.max(scores, axis=-1, keepdims=True))
    expo = jnp.exp(scores - top)
    weights = (expo / lax.optimization_barrier(jnp.sum(expo, axis=-1, keepdims=True))).astype(jnp.bfloat16)
    out = jnp.einsum('grpk,kgd->pgrd', weights.astype(jnp.float32), v_heads)
    return out.reshape(patches, HEADS * HEAD).astype(jnp.bfloat16)

def reference(frames, gain_time, wq_time, wkv_time, wo_time, gain_space, wq_space, wkv_space, wo_space, gain_mlp, w_in, w_out):
    total = frames.shape[0]
    span = 2 * WINDOW + 1
    normed = layer_norm(frames, gain_time)
    queries = project(normed, wq_time).astype(jnp.bfloat16)
    keyvals = project(normed, wkv_time).astype(jnp.bfloat16)
    padded = jnp.pad(keyvals, ((WINDOW, WINDOW), (0, 0), (0, 0)))

    def one_frame(index):
        keys = lax.dynamic_slice_in_dim(padded, index, span, 0)
        where = index + jnp.arange(span, dtype=jnp.int32) - WINDOW
        valid = (where >= 0) & (where < total)
        query = lax.dynamic_index_in_dim(queries, index, 0, False)
        return attend_time(query, keys, valid)
    attended = lax.map(one_frame, jnp.arange(total, dtype=jnp.int32))
    after_time = (frames.astype(jnp.float32) + project(attended, wo_time)).astype(jnp.bfloat16)
    normed = layer_norm(after_time, gain_space)
    queries = project(normed, wq_space).astype(jnp.bfloat16)
    keyvals = project(normed, wkv_space).astype(jnp.bfloat16)
    attended = lax.map(lambda pair: attend_space(pair[0], pair[1]), (queries, keyvals))
    after_space = (after_time.astype(jnp.float32) + project(attended, wo_space)).astype(jnp.bfloat16)
    normed = layer_norm(after_space, gain_mlp)
    hidden = jax.nn.gelu(project(normed, w_in), approximate=True).astype(jnp.bfloat16)
    return (after_space.astype(jnp.float32) + project(hidden, w_out)).astype(jnp.bfloat16)
```

```python
import functools

import jax
import jax.numpy as jnp
from jax import lax
from jax.experimental import pallas as pl
from jax.experimental.pallas import tpu as pltpu
from jax.sharding import PartitionSpec as P

HEADS = 12
KV_HEADS = 4
HEAD = 64
WINDOW = 8
GROUP = HEADS // KV_HEADS
PAIRS = KV_HEADS // 2
PAIR = 2 * HEAD
KV_HALF = KV_HEADS * HEAD
PATCH = 8
BLOCK = 4
ORDER = (1, 2, 0, 3)
HOSTED = (3, 3, 2, 1)
SCALE = HEAD ** -0.5 * 1.4426950408889634
BIG = -1e30
UNROLL = 8
BF = jnp.bfloat16
F32 = jnp.float32
MESH = pl.DeviceIdType.MESH


def mm(a, b):
    return jnp.dot(a, b, preferred_element_type=F32)


def mm_t(a, b):
    return lax.dot_general(a, b, (((1,), (1,)), ((), ())), preferred_element_type=F32)


def norm(x, gain):
    mean = jnp.mean(x, axis=-1, keepdims=True)
    diff = x - mean
    var = jnp.mean(diff * diff, axis=-1, keepdims=True)
    return diff * lax.rsqrt(var + 1e-06) * gain


def attend(jobs, q_ext=None, k_ext=None):
    low = lax.broadcasted_iota(jnp.int32, jobs[0][1].shape, 1) < HEAD
    scores, weights, sums, results = [], [], [], []
    for q, k, _ in jobs:
        zero = jnp.zeros_like(k)
        if q_ext is not None:
            q = jnp.concatenate([q, q_ext], axis=1)
        for kh in (jnp.where(low, k, zero), jnp.where(low, zero, k)):
            if k_ext is not None:
                kh = jnp.concatenate([kh, k_ext], axis=1)
            scores.append(mm_t(q, kh))
    for s in scores:
        weights.append(jnp.exp2(s - jnp.max(s, axis=-1, keepdims=True)).astype(BF))
    for n, (_, _, v) in enumerate(jobs):
        one = jnp.ones_like(v)
        sums.append(mm(weights[2 * n], jnp.where(low, v, one)))
        sums.append(mm(weights[2 * n + 1], jnp.where(low, one, v)))
    low = lax.broadcasted_iota(jnp.int32, sums[0].shape, 1) < HEAD
    for n in range(len(jobs)):
        first, second = sums[2 * n], sums[2 * n + 1]
        total = pltpu.roll(jnp.where(low, second, first), HEAD, 1)
        results.append((jnp.where(low, first, second) / total).astype(BF))
    return results


def gelu_mlp(normed, win_ref, wout_ref):
    ff = win_ref.shape[1]
    step = ff // 4
    out = None
    for i in range(0, ff, step):
        hidden = jax.nn.gelu(mm(normed, win_ref[:, i : i + step]), approximate=True).astype(BF)
        y = mm(hidden, wout_ref[i : i + step, :])
        out = y if out is None else out + y
    return out


def pair_order():
    return [(p * 2 + b) * GROUP + j for p in range(PAIRS) for j in range(GROUP) for b in range(2)]


def pair_columns(src, dst):
    order = pair_order()
    for i in range(0, HEADS, 2):
        halves = [src[:, h * HEAD : (h + 1) * HEAD] for h in order[i : i + 2]]
        dst[:, i * HEAD : (i + 2) * HEAD] = jnp.concatenate(halves, axis=1)


def kernel(
    shards,
    x_hbm, gt_ref, wqt_hbm, wkvt_hbm, wot_hbm, gs_ref, wqs_hbm, wkvs_hbm, wos_hbm, gm_ref, win_hbm, wout_hbm,
    out_hbm,
    x, raw, wqt, wkvt, wot, wqs, wkvs, wos, win, wout,
    q, kv, before, behind, attn, after, gathered, q_ext, k_ext, outs,
    q_in, host_out,
    x_sem, in_sem, row_sem, out_sem, halo_send, halo_recv, right_send, left_send, left_recv, right_recv,
    q_send, q_recv, back_send, back_recv,
):
    count, patches, d = x.shape
    tm, size = lax.axis_index("tm"), lax.axis_size("tm")
    me = lax.axis_index("space")
    groups = patches // PATCH
    blocks = count // BLOCK
    rows = BLOCK * patches
    tile = BLOCK * PATCH
    reach = WINDOW * PATCH
    is_end = (me == 0) | (me == shards - 1)
    is_host = (me == 1) | (me == shards - 2)
    right_is_end = (me > 0) & (me == shards - 2)
    left_is_end = (me < shards - 1) & (me == 1)
    nxt, prv = lax.rem(tm + 1, size), lax.rem(tm + size - 1, size)
    hosted = HOSTED if shards >= 4 else (0,) * blocks

    def frames_of(ref, c):
        return ref.at[c * BLOCK : (c + 1) * BLOCK]

    x_loads = [pltpu.make_async_copy(frames_of(x_hbm, c), frames_of(x, c), x_sem.at[c]) for c in range(blocks)]
    loads = [
        pltpu.make_async_copy(s, t, in_sem.at[i])
        for i, (s, t) in enumerate((
            (wkvt_hbm, wkvt), (wqt_hbm, raw.at[0]), (wqs_hbm, raw.at[1]),
            (wkvs_hbm, wkvs), (win_hbm, win), (wout_hbm, wout),
        ))
    ]
    heads = pair_order()

    def rows_in(src, dst, n):
        return [
            pltpu.make_async_copy(
                src.at[h * HEAD : (h + 1) * HEAD], dst.at[i * HEAD : (i + 1) * HEAD], row_sem.at[n, i]
            )
            for i, h in enumerate(heads)
        ]

    wo_loads = [rows_in(wot_hbm, wot, 0), rows_in(wos_hbm, wos, 1)]
    edges = (blocks - 1, 0, blocks - 2, 1)
    x_loads[edges[0]].start()
    loads[0].start()
    for c in edges[1:]:
        x_loads[c].start()
    loads[1].start()
    for c in wo_loads[0]:
        c.start()
    for c in loads[2:4]:
        c.start()

    barrier = pltpu.get_barrier_semaphore()
    for other in (nxt, prv):
        pl.semaphore_signal(barrier, inc=1, device_id={"tm": other}, device_id_type=MESH)

    @pl.when(me > 0)
    def _():
        pl.semaphore_signal(barrier, inc=1, device_id={"space": me - 1}, device_id_type=MESH)

    @pl.when(me < shards - 1)
    def _():
        pl.semaphore_signal(barrier, inc=1, device_id={"space": me + 1}, device_id_type=MESH)

    gt, gs, gm = gt_ref[...], gs_ref[...], gm_ref[...]

    def halo_copy(side, far):
        if side == 0:
            lo = (count - WINDOW + (0 if far else BLOCK)) * PATCH
            src, dst = kv.at[:, lo : lo + tile], before.at[:, (0 if far else tile) : (tile if far else 2 * tile)]
        else:
            lo = tile if far else 0
            src, dst = kv.at[:, lo : lo + tile], behind.at[:, lo : lo + tile]
        return pltpu.make_async_remote_copy(
            src_ref=src, dst_ref=dst, send_sem=halo_send.at[side, far], recv_sem=halo_recv.at[side, far],
            device_id={"tm": nxt if side == 0 else prv}, device_id_type=MESH,
        )

    halos = [[halo_copy(side, far) for far in range(2)] for side in range(2)]

    def by_group(v):
        return jnp.concatenate(
            [v[f * patches + g * PATCH : f * patches + (g + 1) * PATCH] for g in range(groups) for f in range(BLOCK)], axis=0
        )

    def by_frame(v):
        return jnp.concatenate(
            [v[g * tile + f * PATCH : g * tile + (f + 1) * PATCH] for f in range(BLOCK) for g in range(groups)], axis=0
        )

    for n, c in enumerate(edges):
        x_loads[c].wait()
        normed = by_group(norm(x[c * BLOCK : (c + 1) * BLOCK].reshape(rows, d).astype(F32), gt)).astype(BF)
        attn[c] = normed
        if n == 0:
            loads[0].wait()
        y = mm(normed, wkvt[...]).astype(BF)
        for g in range(groups):
            kv[g, c * tile : (c + 1) * tile] = y[g * tile : (g + 1) * tile]
        if n == 0:
            inner = (me > 0) & (me < shards - 1)

            @pl.when(inner)
            def _():
                pl.semaphore_wait(barrier, 4)

            @pl.when(jnp.logical_not(inner))
            def _():
                pl.semaphore_wait(barrier, 3)

        halos[n % 2][n // 2].start()

    row = lax.broadcasted_iota(jnp.int32, q_ext.shape, 0)
    col = lax.broadcasted_iota(jnp.int32, q_ext.shape, 1)
    hot = (col == row % PATCH) | (col == PATCH + row // PATCH % BLOCK) | (col == PATCH + BLOCK)
    q_ext[...] = jnp.where(hot, 1.0, 0.0).astype(BF)
    row = lax.broadcasted_iota(jnp.int32, k_ext.shape[1:], 0)
    col = lax.broadcasted_iota(jnp.int32, k_ext.shape[1:], 1)
    key_frame, query_frame = row // PATCH, col - PATCH
    off = (col < PATCH) & (col != row % PATCH)
    off = off | (
        (query_frame >= 0) & (query_frame < BLOCK)
        & ((key_frame < query_frame) | (key_frame > query_frame + 2 * WINDOW))
    )
    for c in range(blocks):
        frame = key_frame + (tm * count + c * BLOCK - WINDOW)
        outside = (query_frame == BLOCK) & ((frame < 0) | (frame >= size * count))
        k_ext[c] = jnp.where(off | outside, BIG, 0.0).astype(BF)

    loads[1].wait()
    pair_columns(raw.at[0], wqt)
    for c in ORDER:
        q[c] = (mm(attn[c], wqt[...]) * SCALE).astype(BF)
    loads[2].wait()
    pair_columns(raw.at[1], wqs)
    for c in wo_loads[1] + loads[4:]:
        c.start()

    pieces, of_step = [], []
    for i, c in enumerate(ORDER):
        h = hosted[i]
        of_step.append([])
        for lo, n, away in ((0, h, True), (h, BLOCK - h, False)):
            if n:
                of_step[i].append(len(pieces))
                pieces.append((c, lo, n, away))

    def piece(shard, p):
        c, lo, n, _ = pieces[p]
        return gathered.at[shard, c, lo * patches : (lo + n) * patches]

    def margin(p):
        return 2 if pieces[p][3] else 1

    def to_right(p, dist):
        return pltpu.make_async_remote_copy(
            src_ref=piece(me - dist, p), dst_ref=piece(me - dist, p),
            send_sem=right_send.at[p, dist], recv_sem=left_recv.at[p, dist],
            device_id={"space": me + 1}, device_id_type=MESH,
        )

    def to_left(p, dist):
        return pltpu.make_async_remote_copy(
            src_ref=piece(me + dist, p), dst_ref=piece(me + dist, p),
            send_sem=left_send.at[p, dist], recv_sem=right_recv.at[p, dist],
            device_id={"space": me - 1}, device_id_type=MESH,
        )

    def sends_right(p, dist):
        return (me - dist >= 0) & (me + margin(p) < shards)

    def sends_left(p, dist):
        return (me + dist < shards) & (me >= margin(p))

    def start_if(cond, copy):
        @pl.when(cond)
        def _():
            copy().start()

    def query_copy(i, step):
        at = (ORDER[i], slice(0, hosted[i] * patches))
        return pltpu.make_async_remote_copy(
            src_ref=q.at[at], dst_ref=q_in.at[at], send_sem=q_send.at[i], recv_sem=q_recv.at[i],
            device_id={"space": me + step}, device_id_type=MESH,
        )

    def back_copy(i, step):
        at = (ORDER[i], slice(0, hosted[i] * patches))
        return pltpu.make_async_remote_copy(
            src_ref=host_out.at[at], dst_ref=attn.at[at], send_sem=back_send.at[i], recv_sem=back_recv.at[i],
            device_id={"space": me + step}, device_id_type=MESH,
        )

    def on(position, action):
        @pl.when(me == position)
        def _():
            action()

    def send_early(i):
        for p in of_step[i]:
            if not pieces[p][3]:
                start_if(right_is_end, lambda: to_right(p, 0))
                start_if(left_is_end, lambda: to_left(p, 0))

    def send_own(i):
        for p in of_step[i]:
            start_if(sends_right(p, 0) & jnp.logical_not(right_is_end), lambda: to_right(p, 0))
            start_if(sends_left(p, 0) & jnp.logical_not(left_is_end), lambda: to_left(p, 0))

    def send_queries(i):
        if hosted[i]:
            on(0, lambda: query_copy(i, 1).start())
            on(shards - 1, lambda: query_copy(i, -1).start())

    def forward(i, dist):
        for p in of_step[i]:
            @pl.when((me - dist >= 0) & (me + margin(p) - 1 < shards))
            def _():
                pltpu.make_async_remote_copy(
                    src_ref=piece(me - dist, p), dst_ref=piece(me - dist, p),
                    send_sem=right_send.at[p, dist - 1], recv_sem=left_recv.at[p, dist - 1],
                    device_id={"space": me - 1}, device_id_type=MESH,
                ).wait_recv()

            if dist < shards - 1:
                start_if(sends_right(p, dist), lambda: to_right(p, dist))

            @pl.when((me + dist < shards) & (me >= margin(p) - 1))
            def _():
                pltpu.make_async_remote_copy(
                    src_ref=piece(me + dist, p), dst_ref=piece(me + dist, p),
                    send_sem=left_send.at[p, dist - 1], recv_sem=right_recv.at[p, dist - 1],
                    device_id={"space": me + 1}, device_id_type=MESH,
                ).wait_recv()

            if dist < shards - 1:
                start_if(sends_left(p, dist), lambda: to_left(p, dist))

    def time_attention(c):
        lo = c * tile - reach
        hi = lo + tile + 2 * reach
        own = blocks * tile

        for first in range(0, groups, UNROLL):
            jobs = []
            for g in range(first, first + UNROLL):
                parts = [kv[g, max(lo, 0) : min(hi, own)]]
                if lo < 0:
                    parts.insert(0, before[g, reach + lo :])
                if hi > own:
                    parts.append(behind[g, : hi - own])
                keys = jnp.concatenate(parts, axis=0)
                at = slice(g * tile, (g + 1) * tile)
                for pair in range(PAIRS):
                    base = pair * GROUP * PAIR
                    qs = [q[c, at, base + j * PAIR : base + (j + 1) * PAIR] for j in range(GROUP)]
                    k = keys[:, pair * PAIR : (pair + 1) * PAIR]
                    v = keys[:, KV_HALF + pair * PAIR : KV_HALF + (pair + 1) * PAIR]
                    jobs.append((jnp.concatenate(qs, axis=0), k, v))
            results = attend(jobs, q_ext[...], k_ext[c])
            for u in range(UNROLL):
                at = slice((first + u) * tile, (first + u + 1) * tile)
                for pair in range(PAIRS):
                    base = pair * GROUP * PAIR
                    for j in range(GROUP):
                        attn[c, at, base + j * PAIR : base + (j + 1) * PAIR] = results[u * PAIRS + pair][j * tile : (j + 1) * tile]

    halo_order = ((0, 0), (1, 0), (0, 1), (1, 1))
    for i, c in enumerate(ORDER):
        halos[halo_order[i][0]][halo_order[i][1]].wait_recv()
        time_attention(c)
        if i == 0:
            for w in wo_loads[0] + loads[3:4]:
                w.wait()
        if i == 2:
            forward(0, 1)
            send_own(1)
            send_queries(1)
        y = by_frame(mm(attn[c], wot[...]))
        res = (x[c * BLOCK : (c + 1) * BLOCK].reshape(rows, d).astype(F32) + y).astype(BF)
        after[c] = res
        normed = norm(res.astype(F32), gs).astype(BF)
        gathered[me, c] = mm(normed, wkvs[...]).astype(BF)
        send_early(i)
        if i == 0:
            send_own(i)
        q[c] = (mm(normed, wqs[...]) * SCALE).astype(BF)
        if i == 0:
            send_queries(i)

    def space_attention(c, start, stop, both):
        sources = ((q, attn), (q_in, host_out)) if both else ((q, attn),)
        width = 1 if both else 2
        for first in range(start, stop, width):
            frames = range(first, min(first + width, stop))
            jobs = []
            for f in frames:
                at = slice(f * patches, (f + 1) * patches)
                for pair in range(PAIRS):
                    base = pair * GROUP * PAIR
                    k = gathered[:, c, at, pair * PAIR : (pair + 1) * PAIR].reshape(shards * patches, PAIR)
                    v = gathered[:, c, at, KV_HALF + pair * PAIR : KV_HALF + (pair + 1) * PAIR].reshape(shards * patches, PAIR)
                    qs = [s[c, at, base + j * PAIR : base + (j + 1) * PAIR] for s, _ in sources for j in range(GROUP)]
                    jobs.append((jnp.concatenate(qs, axis=0), k, v))
            results = attend(jobs)
            for u, f in enumerate(frames):
                at = slice(f * patches, (f + 1) * patches)
                for pair in range(PAIRS):
                    base = pair * GROUP * PAIR
                    o = results[u * PAIRS + pair]
                    for n, (_, target) in enumerate(sources):
                        for j in range(GROUP):
                            m = n * GROUP + j
                            target[c, at, base + j * PAIR : base + (j + 1) * PAIR] = o[m * patches : (m + 1) * patches]

    for w in wo_loads[1] + loads[4:]:
        w.wait()
    writes = []
    for i, c in enumerate(ORDER):
        for dist in range(2, shards):
            forward(i, dist)
        h = hosted[i]
        if h:
            @pl.when(is_host)
            def _():
                on(1, lambda: query_copy(i, -1).wait_recv())
                on(shards - 2, lambda: query_copy(i, 1).wait_recv())
                space_attention(c, 0, h, True)

            on(1, lambda: back_copy(i, -1).start())
            on(shards - 2, lambda: back_copy(i, 1).start())
            if shards > 4:
                @pl.when(jnp.logical_not(is_host | is_end))
                def _():
                    space_attention(c, 0, h, False)

        if i + 1 < blocks:
            forward(i + 1, 1)
        if i + 2 < blocks:
            send_own(i + 2)
            send_queries(i + 2)
        if h < BLOCK:
            space_attention(c, h, BLOCK, False)
        if h:
            on(0, lambda: back_copy(i, 1).wait_recv())
            on(shards - 1, lambda: back_copy(i, -1).wait_recv())
        y = mm(attn[c], wos[...])
        res = (after[c].astype(F32) + y).astype(BF)
        normed = norm(res.astype(F32), gm).astype(BF)
        y = (res.astype(F32) + gelu_mlp(normed, win, wout)).astype(BF)
        outs[c * BLOCK : (c + 1) * BLOCK] = y.reshape(BLOCK, patches, d)
        write = pltpu.make_async_copy(frames_of(outs, c), frames_of(out_hbm, c), out_sem.at[c])
        write.start()
        writes.append(write)

    for w in writes:
        w.wait()
    for side in range(2):
        for c in halos[side]:
            c.wait_send()
    for p in range(len(pieces)):
        for dist in range(shards - 1):
            @pl.when(sends_right(p, dist))
            def _():
                to_right(p, dist).wait_send()

            @pl.when(sends_left(p, dist))
            def _():
                to_left(p, dist).wait_send()

    for i in range(blocks):
        if hosted[i]:
            on(0, lambda: query_copy(i, 1).wait_send())
            on(shards - 1, lambda: query_copy(i, -1).wait_send())
            on(1, lambda: back_copy(i, -1).wait_send())
            on(shards - 2, lambda: back_copy(i, 1).wait_send())


def body(*args):
    frames = args[0]
    count, patches, d = frames.shape
    kvw = args[3].shape[1]
    ff = args[10].shape[1]
    shards = lax.axis_size("space")
    blocks = count // BLOCK
    groups = patches // PATCH
    rows = BLOCK * patches
    keys = (BLOCK + 2 * WINDOW) * PATCH
    hbm = pl.BlockSpec(memory_space=pl.ANY)
    vmem = pl.BlockSpec(memory_space=pltpu.VMEM)
    dma = pltpu.SemaphoreType.DMA
    return pl.pallas_call(
        functools.partial(kernel, shards),
        in_specs=[hbm, vmem, hbm, hbm, hbm, vmem, hbm, hbm, hbm, vmem, hbm, hbm],
        out_specs=hbm,
        out_shape=jax.ShapeDtypeStruct(frames.shape, BF),
        scratch_shapes=[
            pltpu.VMEM((count, patches, d), BF),
            pltpu.VMEM((2, d, d), BF),
            pltpu.VMEM((d, d), BF),
            pltpu.VMEM((d, kvw), BF),
            pltpu.VMEM((d, d), BF),
            pltpu.VMEM((d, d), BF),
            pltpu.VMEM((d, kvw), BF),
            pltpu.VMEM((d, d), BF),
            pltpu.VMEM((d, ff), BF),
            pltpu.VMEM((ff, d), BF),
            pltpu.VMEM((blocks, rows, d), BF),
            pltpu.VMEM((groups, count * PATCH, kvw), BF),
            pltpu.VMEM((groups, WINDOW * PATCH, kvw), BF),
            pltpu.VMEM((groups, WINDOW * PATCH, kvw), BF),
            pltpu.VMEM((blocks, rows, d), BF),
            pltpu.VMEM((blocks, rows, d), BF),
            pltpu.VMEM((shards, blocks, rows, kvw), BF),
            pltpu.VMEM((GROUP * BLOCK * PATCH, PAIR), BF),
            pltpu.VMEM((blocks, keys, PAIR), BF),
            pltpu.VMEM((count, patches, d), BF),
            pltpu.VMEM((blocks, rows, d), BF),
            pltpu.VMEM((blocks, rows, d), BF),
            dma((blocks,)),
            dma((6,)),
            dma((2, HEADS)),
            dma((blocks,)),
            dma((2, 2)),
            dma((2, 2)),
            dma((2 * blocks, shards)),
            dma((2 * blocks, shards)),
            dma((2 * blocks, shards)),
            dma((2 * blocks, shards)),
            dma((blocks,)),
            dma((blocks,)),
            dma((blocks,)),
            dma((blocks,)),
        ],
        compiler_params=pltpu.CompilerParams(
            vmem_limit_bytes=60 << 20, collective_id=0, has_side_effects=True
        ),
        name="encoder_block",
    )(*args)


def solution(mesh):
    in_specs = (P("tm", "space", None),) + (P(),) * 11
    out_specs = P("tm", "space", None)
    return jax.shard_map(body, mesh=mesh, in_specs=in_specs, out_specs=out_specs, check_vma=False)
```

```python
import functools

import jax
import jax.numpy as jnp
from jax import lax
from jax.experimental import pallas as pl
from jax.experimental.pallas import tpu as pltpu
from jax.sharding import PartitionSpec as P

HEADS = 12
KV_HEADS = 4
HEAD = 64
WINDOW = 8
GROUP = HEADS // KV_HEADS
PAIRS = KV_HEADS // 2
PAIR = 2 * HEAD
KV_HALF = KV_HEADS * HEAD
PATCH = 8
BLOCK = 4
ORDER = (1, 2, 0, 3)
UNITS = ((0, 0, 2, 1), (0, 2, 4, 1), (1, 0, 2, 1), (1, 2, 4, 1), (2, 0, 2, 1), (2, 2, 4, 1), (3, 0, 2, 1), (3, 2, 4, 1))
SCALE = HEAD ** -0.5 * 1.4426950408889634
BIG = -1e30
UNROLL = 8
COPIES = 4
BF = jnp.bfloat16
F32 = jnp.float32
MESH = pl.DeviceIdType.MESH


def mm(a, b):
    return jnp.dot(a, b, preferred_element_type=F32)


def mm_t(a, b):
    return lax.dot_general(a, b, (((1,), (1,)), ((), ())), preferred_element_type=F32)


def norm(x, gain):
    mean = jnp.mean(x, axis=-1, keepdims=True)
    diff = x - mean
    var = jnp.mean(diff * diff, axis=-1, keepdims=True)
    return diff * lax.rsqrt(var + 1e-06) * gain


def attend(jobs, q_ext=None, k_ext=None):
    low = lax.broadcasted_iota(jnp.int32, jobs[0][1].shape, 1) < HEAD
    scores, weights, sums, results = [], [], [], []
    for q, k, _ in jobs:
        zero = jnp.zeros_like(k)
        if q_ext is not None:
            q = jnp.concatenate([q, q_ext], axis=1)
        for kh in (jnp.where(low, k, zero), jnp.where(low, zero, k)):
            if k_ext is not None:
                kh = jnp.concatenate([kh, k_ext], axis=1)
            scores.append(mm_t(q, kh))
    for s in scores:
        weights.append(jnp.exp2(s - jnp.max(s, axis=-1, keepdims=True)).astype(BF))
    for n, (_, _, v) in enumerate(jobs):
        one = jnp.ones_like(v)
        sums.append(mm(weights[2 * n], jnp.where(low, v, one)))
        sums.append(mm(weights[2 * n + 1], jnp.where(low, one, v)))
    low = lax.broadcasted_iota(jnp.int32, sums[0].shape, 1) < HEAD
    for n in range(len(jobs)):
        first, second = sums[2 * n], sums[2 * n + 1]
        total = pltpu.roll(jnp.where(low, second, first), HEAD, 1)
        results.append((jnp.where(low, first, second) / total).astype(BF))
    return results


def gelu_mlp(normed, win_ref, wout_ref):
    ff = win_ref.shape[1]
    step = ff // 4
    out = None
    for i in range(0, ff, step):
        hidden = jax.nn.gelu(mm(normed, win_ref[:, i : i + step]), approximate=True).astype(BF)
        y = mm(hidden, wout_ref[i : i + step, :])
        out = y if out is None else out + y
    return out


def pair_order():
    return [(p * 2 + b) * GROUP + j for p in range(PAIRS) for j in range(GROUP) for b in range(2)]


def pair_columns(src, dst):
    order = pair_order()
    for i in range(0, HEADS, 2):
        halves = [src[:, h * HEAD : (h + 1) * HEAD] for h in order[i : i + 2]]
        dst[:, i * HEAD : (i + 2) * HEAD] = jnp.concatenate(halves, axis=1)


def kernel(
    shards,
    x_hbm, gt_ref, wqt_hbm, wkvt_hbm, wot_hbm, gs_ref, wqs_hbm, wkvs_hbm, wos_hbm, gm_ref, win_hbm, wout_hbm,
    out_hbm,
    x, raw, wqt, wkvt, wot, wqs, wkvs, wos, win, wout,
    q, kv, attn, after, gathered, q_ext, k_ext, outs,
    q_in, host_out,
    x_sem, in_sem, row_sem, out_sem, halo_send, halo_recv, right_send, left_send, left_recv, right_recv,
    q_send, q_recv, back_send, back_recv,
):
    count, patches, d = x.shape
    tm, size = lax.axis_index("tm"), lax.axis_size("tm")
    me = lax.axis_index("space")
    groups = patches // PATCH
    blocks = count // BLOCK
    rows = BLOCK * patches
    tile = BLOCK * PATCH
    reach = WINDOW * PATCH
    is_end = (me == 0) | (me == shards - 1)
    is_host = (me == 1) | (me == shards - 2)
    right_is_end = (me > 0) & (me == shards - 2)
    left_is_end = (me < shards - 1) & (me == 1)
    nxt, prv = lax.rem(tm + 1, size), lax.rem(tm + size - 1, size)
    first_core = lax.rem(tm, 2) == 0
    order = [jnp.where(first_core, blocks - 1 - c, c) for c in ORDER]
    units = [(i, order[i], lo, hi, h if shards >= 4 else 0) for i, lo, hi, h in UNITS]

    def frames_of(ref, c):
        return ref.at[c * BLOCK : (c + 1) * BLOCK]

    def own_halo(side, far):
        @pl.when(first_core)
        def _():
            halos[1 - side][far].wait_recv()

        @pl.when(jnp.logical_not(first_core))
        def _():
            halos[side][far].wait_recv()

    x_loads = [pltpu.make_async_copy(frames_of(x_hbm, c), frames_of(x, c), x_sem.at[c]) for c in range(blocks)]
    loads = [
        pltpu.make_async_copy(s, t, in_sem.at[i])
        for i, (s, t) in enumerate((
            (wkvt_hbm, wkvt), (wqt_hbm, raw.at[0]), (wqs_hbm, raw.at[1]),
            (wkvs_hbm, wkvs), (win_hbm, win), (wout_hbm, wout),
        ))
    ]
    heads = pair_order()

    def rows_in(src, dst, n):
        return [
            pltpu.make_async_copy(
                src.at[h * HEAD : (h + 1) * HEAD], dst.at[i * HEAD : (i + 1) * HEAD], row_sem.at[n, i]
            )
            for i, h in enumerate(heads)
        ]

    wo_loads = [rows_in(wot_hbm, wot, 0), rows_in(wos_hbm, wos, 1)]
    edges = (blocks - 1, 0, blocks - 2, 1)
    x_loads[edges[0]].start()
    loads[0].start()
    for c in edges[1:]:
        x_loads[c].start()
    loads[1].start()
    for c in wo_loads[0]:
        c.start()
    for c in loads[2:4]:
        c.start()

    barrier = pltpu.get_barrier_semaphore()
    for other in (nxt, prv):
        pl.semaphore_signal(barrier, inc=1, device_id={"tm": other}, device_id_type=MESH)

    @pl.when(me > 0)
    def _():
        pl.semaphore_signal(barrier, inc=1, device_id={"space": me - 1}, device_id_type=MESH)

    @pl.when(me < shards - 1)
    def _():
        pl.semaphore_signal(barrier, inc=1, device_id={"space": me + 1}, device_id_type=MESH)

    gt, gs, gm = gt_ref[...], gs_ref[...], gm_ref[...]

    def halo_copy(side, far):
        if side == 0:
            lo, to = reach + count * PATCH - (2 if far else 1) * tile, 0 if far else tile
        else:
            lo = reach + (tile if far else 0)
            to = lo + count * PATCH
        return pltpu.make_async_remote_copy(
            src_ref=kv.at[:, lo : lo + tile], dst_ref=kv.at[:, to : to + tile], send_sem=halo_send.at[side, far], recv_sem=halo_recv.at[side, far],
            device_id={"tm": nxt if side == 0 else prv}, device_id_type=MESH,
        )

    halos = [[halo_copy(side, far) for far in range(2)] for side in range(2)]

    def by_group(v):
        return jnp.concatenate(
            [v[f * patches + g * PATCH : f * patches + (g + 1) * PATCH] for g in range(groups) for f in range(BLOCK)], axis=0
        )

    def by_frame(v):
        return jnp.concatenate(
            [v[g * tile + f * PATCH : g * tile + (f + 1) * PATCH] for f in range(BLOCK) for g in range(groups)], axis=0
        )

    row = lax.broadcasted_iota(jnp.int32, q_ext.shape, 0)
    col = lax.broadcasted_iota(jnp.int32, q_ext.shape, 1)
    hot = (col == row % PATCH) | (col == PATCH + row // PATCH % BLOCK) | (col == PATCH + BLOCK)
    q_ext[...] = jnp.where(hot, 1.0, 0.0).astype(BF)
    row = lax.broadcasted_iota(jnp.int32, k_ext.shape[1:], 0)
    col = lax.broadcasted_iota(jnp.int32, k_ext.shape[1:], 1)
    key_frame, query_frame = row // PATCH, col - PATCH
    off = (col < PATCH) & (col != row % PATCH)
    off = off | (
        (query_frame >= 0) & (query_frame < BLOCK)
        & ((key_frame < query_frame) | (key_frame > query_frame + 2 * WINDOW))
    )
    for c in range(blocks):
        frame = key_frame + (tm * count + c * BLOCK - WINDOW)
        outside = (query_frame == BLOCK) & ((frame < 0) | (frame >= size * count))
        k_ext[c] = jnp.where(off | outside, BIG, 0.0).astype(BF)

    for n, c in enumerate(edges):
        x_loads[c].wait()
        normed = by_group(norm(x[c * BLOCK : (c + 1) * BLOCK].reshape(rows, d).astype(F32), gt)).astype(BF)
        attn[c] = normed
        if n == 0:
            loads[0].wait()
        y = mm(normed, wkvt[...]).astype(BF)
        for g in range(groups):
            kv[g, reach + c * tile : reach + (c + 1) * tile] = y[g * tile : (g + 1) * tile]
        if n == 0:
            inner = (me > 0) & (me < shards - 1)

            @pl.when(inner)
            def _():
                pl.semaphore_wait(barrier, 4)

            @pl.when(jnp.logical_not(inner))
            def _():
                pl.semaphore_wait(barrier, 3)

        halos[n % 2][n // 2].start()

    loads[1].wait()
    pair_columns(raw.at[0], wqt)
    q[order[0]] = (mm(attn[order[0]], wqt[...]) * SCALE).astype(BF)
    for c in wo_loads[1] + loads[4:]:
        c.start()

    pieces, of_unit = [], []
    for _, c, lo, hi, h in units:
        mine = [(lo, h, True)] * (h > 0) + [(f, 1, False) for f in range(lo + h, hi)]
        of_unit.append(list(range(len(pieces), len(pieces) + len(mine))))
        pieces.extend((c,) + m for m in mine)

    def piece(shard, p):
        c, lo, n, _ = pieces[p]
        return gathered.at[shard, c, lo * patches : (lo + n) * patches]

    def margin(p):
        return 2 if pieces[p][3] else 1

    def to_right(p, dist):
        return pltpu.make_async_remote_copy(
            src_ref=piece(me - dist, p), dst_ref=piece(me - dist, p),
            send_sem=right_send.at[p, dist], recv_sem=left_recv.at[p, dist],
            device_id={"space": me + 1}, device_id_type=MESH,
        )

    def to_left(p, dist):
        return pltpu.make_async_remote_copy(
            src_ref=piece(me + dist, p), dst_ref=piece(me + dist, p),
            send_sem=left_send.at[p, dist], recv_sem=right_recv.at[p, dist],
            device_id={"space": me - 1}, device_id_type=MESH,
        )

    def sends_right(p, dist):
        return (me - dist >= 0) & (me + margin(p) < shards)

    def sends_left(p, dist):
        return (me + dist < shards) & (me >= margin(p))

    def start_if(cond, copy):
        @pl.when(cond)
        def _():
            copy().start()

    def hosted_rows(i):
        _, c, lo, _, h = units[i]
        return c, slice(lo * patches, (lo + h) * patches)

    def query_copy(i, step):
        at = hosted_rows(i)
        return pltpu.make_async_remote_copy(
            src_ref=q.at[at], dst_ref=q_in.at[at], send_sem=q_send.at[i], recv_sem=q_recv.at[i],
            device_id={"space": me + step}, device_id_type=MESH,
        )

    def back_copy(i, step):
        at = hosted_rows(i)
        return pltpu.make_async_remote_copy(
            src_ref=host_out.at[at], dst_ref=attn.at[at], send_sem=back_send.at[i], recv_sem=back_recv.at[i],
            device_id={"space": me + step}, device_id_type=MESH,
        )

    def on(position, action):
        @pl.when(me == position)
        def _():
            action()

    def send_early(i):
        for p in of_unit[i]:
            if not pieces[p][3]:
                start_if(right_is_end, lambda: to_right(p, 0))
                start_if(left_is_end, lambda: to_left(p, 0))

    def send_own(i):
        for p in of_unit[i]:
            start_if(sends_right(p, 0) & jnp.logical_not(right_is_end), lambda: to_right(p, 0))
            start_if(sends_left(p, 0) & jnp.logical_not(left_is_end), lambda: to_left(p, 0))

    def send_queries(i):
        if units[i][4]:
            on(0, lambda: query_copy(i, 1).start())
            on(shards - 1, lambda: query_copy(i, -1).start())

    def forward(i, dist):
        for p in of_unit[i]:
            @pl.when((me - dist >= 0) & (me + margin(p) - 1 < shards))
            def _():
                pltpu.make_async_remote_copy(
                    src_ref=piece(me - dist, p), dst_ref=piece(me - dist, p),
                    send_sem=right_send.at[p, dist - 1], recv_sem=left_recv.at[p, dist - 1],
                    device_id={"space": me - 1}, device_id_type=MESH,
                ).wait_recv()

            if dist < shards - 1:
                start_if(sends_right(p, dist), lambda: to_right(p, dist))

            @pl.when((me + dist < shards) & (me >= margin(p) - 1))
            def _():
                pltpu.make_async_remote_copy(
                    src_ref=piece(me + dist, p), dst_ref=piece(me + dist, p),
                    send_sem=left_send.at[p, dist - 1], recv_sem=right_recv.at[p, dist - 1],
                    device_id={"space": me + 1}, device_id_type=MESH,
                ).wait_recv()

            if dist < shards - 1:
                start_if(sends_left(p, dist), lambda: to_left(p, dist))

    def time_attention(c):
        span = pl.ds(pl.multiple_of(c * tile, tile), tile + 2 * reach)
        for first in range(0, groups, UNROLL):
            jobs = []
            for g in range(first, first + UNROLL):
                keys = kv[g, span]
                at = slice(g * tile, (g + 1) * tile)
                for pair in range(PAIRS):
                    base = pair * GROUP * PAIR
                    qs = [q[c, at, base + j * PAIR : base + (j + 1) * PAIR] for j in range(GROUP)]
                    k = keys[:, pair * PAIR : (pair + 1) * PAIR]
                    v = keys[:, KV_HALF + pair * PAIR : KV_HALF + (pair + 1) * PAIR]
                    jobs.append((jnp.concatenate(qs, axis=0), k, v))
            results = attend(jobs, q_ext[...], k_ext[c])
            for u in range(UNROLL):
                at = slice((first + u) * tile, (first + u + 1) * tile)
                for pair in range(PAIRS):
                    base = pair * GROUP * PAIR
                    for j in range(GROUP):
                        attn[c, at, base + j * PAIR : base + (j + 1) * PAIR] = results[u * PAIRS + pair][j * tile : (j + 1) * tile]

    for i, c in enumerate(order):
        if i:
            q[c] = (mm(attn[c], wqt[...]) * SCALE).astype(BF)
        own_halo(i % 2, i // 2)
        time_attention(c)
        if i == 0:
            for w in wo_loads[0] + loads[3:4]:
                w.wait()
        if i == 2:
            forward(0, 1)
            send_own(2)
            send_queries(2)
        y = by_frame(mm(attn[c], wot[...]))
        res = (x[pl.ds(c * BLOCK, BLOCK)].reshape(rows, d).astype(F32) + y).astype(BF)
        after[c] = res
        normed = norm(res.astype(F32), gs).astype(BF)
        gathered[me, c] = mm(normed, wkvs[...]).astype(BF)
        for n, unit in enumerate(units):
            if unit[0] == i:
                send_early(n)
        if i == 0:
            send_own(0)
            send_own(1)
            loads[2].wait()
            pair_columns(raw.at[1], wqs)
        q[c] = (mm(normed, wqs[...]) * SCALE).astype(BF)
        if i == 0:
            send_queries(0)
            send_queries(1)

    def space_attention(c, start, stop, both):
        sources = ((q, attn), (q_in, host_out)) if both else ((q, attn),)
        width = 1 if both else 2
        for first in range(start, stop, width):
            frames = range(first, min(first + width, stop))
            jobs = []
            for f in frames:
                at = slice(f * patches, (f + 1) * patches)
                for pair in range(PAIRS):
                    base = pair * GROUP * PAIR
                    k = gathered[:, c, at, pair * PAIR : (pair + 1) * PAIR].reshape(shards * patches, PAIR)
                    v = gathered[:, c, at, KV_HALF + pair * PAIR : KV_HALF + (pair + 1) * PAIR].reshape(shards * patches, PAIR)
                    qs = [s[c, at, base + j * PAIR : base + (j + 1) * PAIR] for s, _ in sources for j in range(GROUP)]
                    jobs.append((jnp.concatenate(qs, axis=0), k, v))
            results = attend(jobs)
            for u, f in enumerate(frames):
                at = slice(f * patches, (f + 1) * patches)
                for pair in range(PAIRS):
                    base = pair * GROUP * PAIR
                    o = results[u * PAIRS + pair]
                    for n, (_, target) in enumerate(sources):
                        for j in range(GROUP):
                            m = n * GROUP + j
                            target[c, at, base + j * PAIR : base + (j + 1) * PAIR] = o[m * patches : (m + 1) * patches]

    for w in wo_loads[1] + loads[4:]:
        w.wait()
    writes = []
    for i, (_, c, lo, hi, h) in enumerate(units):
        if i + 1 < len(units):
            forward(i + 1, 1)
        if i + 3 < len(units):
            send_own(i + 3)
            send_queries(i + 3)
        for dist in range(2, shards):
            forward(i, dist)
        if h:
            @pl.when(is_host)
            def _():
                on(1, lambda: query_copy(i, -1).wait_recv())
                on(shards - 2, lambda: query_copy(i, 1).wait_recv())
                space_attention(c, lo, lo + h, True)

            on(1, lambda: back_copy(i, -1).start())
            on(shards - 2, lambda: back_copy(i, 1).start())
            if shards > 4:
                @pl.when(jnp.logical_not(is_host | is_end))
                def _():
                    space_attention(c, lo, lo + h, False)

        space_attention(c, lo + h, hi, False)
        if i < len(units) - 2:
            if i % 2 == 0:
                continue
            lo = 0
        for n in range(i - 1 if lo == 0 and hi == BLOCK else i, i + 1):
            if units[n][4]:
                on(0, lambda: back_copy(n, 1).wait_recv())
                on(shards - 1, lambda: back_copy(n, -1).wait_recv())
        at = slice(lo * patches, hi * patches)
        y = mm(attn[c, at], wos[...])
        res = (after[c, at].astype(F32) + y).astype(BF)
        normed = norm(res.astype(F32), gm).astype(BF)
        y = (res.astype(F32) + gelu_mlp(normed, win, wout)).astype(BF)
        at = pl.ds(c * BLOCK + lo, hi - lo)
        outs[at] = y.reshape(hi - lo, patches, d)
        write = pltpu.make_async_copy(outs.at[at], out_hbm.at[at], out_sem.at[len(writes)])
        write.start()
        writes.append(write)

    for w in writes:
        w.wait()
    for side in range(2):
        for c in halos[side]:
            c.wait_send()
    for p in range(len(pieces)):
        for dist in range(shards - 1):
            @pl.when(sends_right(p, dist))
            def _():
                to_right(p, dist).wait_send()

            @pl.when(sends_left(p, dist))
            def _():
                to_left(p, dist).wait_send()

    for i in range(len(units)):
        if units[i][4]:
            on(0, lambda: query_copy(i, 1).wait_send())
            on(shards - 1, lambda: query_copy(i, -1).wait_send())
            on(1, lambda: back_copy(i, -1).wait_send())
            on(shards - 2, lambda: back_copy(i, 1).wait_send())


def copy_kernel(src, dst, held, in_sem, out_sem):
    count = src.shape[0]
    step = count // COPIES
    parts = [pl.ds(i * step, step) for i in range(COPIES)]
    arrive = [pltpu.make_async_copy(src.at[at], held.at[at], in_sem.at[i]) for i, at in enumerate(parts)]
    leave = [pltpu.make_async_copy(held.at[at], dst.at[at], out_sem.at[i]) for i, at in enumerate(parts)]
    for c in arrive:
        c.start()
    for c, after in zip(arrive, leave):
        c.wait()
        after.start()
    for c in leave:
        c.wait()


def body(*args):
    frames = args[0]
    count, patches, d = frames.shape
    kvw = args[3].shape[1]
    ff = args[10].shape[1]
    shards = lax.axis_size("space")
    blocks = count // BLOCK
    groups = patches // PATCH
    rows = BLOCK * patches
    keys = (BLOCK + 2 * WINDOW) * PATCH
    hbm = pl.BlockSpec(memory_space=pl.ANY)
    vmem = pl.BlockSpec(memory_space=pltpu.VMEM)
    dma = pltpu.SemaphoreType.DMA
    encoded = pl.pallas_call(
        functools.partial(kernel, shards),
        in_specs=[hbm, vmem, hbm, hbm, hbm, vmem, hbm, hbm, hbm, vmem, hbm, hbm],
        out_specs=hbm,
        out_shape=jax.ShapeDtypeStruct(frames.shape, BF),
        scratch_shapes=[
            pltpu.VMEM((count, patches, d), BF),
            pltpu.VMEM((2, d, d), BF),
            pltpu.VMEM((d, d), BF),
            pltpu.VMEM((d, kvw), BF),
            pltpu.VMEM((d, d), BF),
            pltpu.VMEM((d, d), BF),
            pltpu.VMEM((d, kvw), BF),
            pltpu.VMEM((d, d), BF),
            pltpu.VMEM((d, ff), BF),
            pltpu.VMEM((ff, d), BF),
            pltpu.VMEM((blocks, rows, d), BF),
            pltpu.VMEM((groups, (count + 2 * WINDOW) * PATCH, kvw), BF),
            pltpu.VMEM((blocks, rows, d), BF),
            pltpu.VMEM((blocks, rows, d), BF),
            pltpu.VMEM((shards, blocks, rows, kvw), BF),
            pltpu.VMEM((GROUP * BLOCK * PATCH, PAIR), BF),
            pltpu.VMEM((blocks, keys, PAIR), BF),
            pltpu.VMEM((count, patches, d), BF),
            pltpu.VMEM((blocks, rows, d), BF),
            pltpu.VMEM((blocks, rows, d), BF),
            dma((blocks,)),
            dma((6,)),
            dma((2, HEADS)),
            dma((len(UNITS),)),
            dma((2, 2)),
            dma((2, 2)),
            dma((count, shards)),
            dma((count, shards)),
            dma((count, shards)),
            dma((count, shards)),
            dma((len(UNITS),)),
            dma((len(UNITS),)),
            dma((len(UNITS),)),
            dma((len(UNITS),)),
        ],
        compiler_params=pltpu.CompilerParams(
            vmem_limit_bytes=60 << 20, collective_id=0, has_side_effects=True
        ),
        name="encoder_block",
    )(*args)
    return pl.pallas_call(
        copy_kernel,
        in_specs=[hbm],
        out_specs=hbm,
        out_shape=jax.ShapeDtypeStruct(frames.shape, BF),
        scratch_shapes=[pltpu.VMEM(frames.shape, BF), dma((COPIES,)), dma((COPIES,))],
        name="write_out",
    )(encoded)


def solution(mesh):
    in_specs = (P("tm", "space", None),) + (P(),) * 11
    out_specs = P("tm", "space", None)
    return jax.shard_map(body, mesh=mesh, in_specs=in_specs, out_specs=out_specs, check_vma=False)
```
